32 devices in a mesh: ctx: 8 (over z, x), heads: 4 (over y, core).
Axes of the slice: x: 2, y: 2, z: 4, core: 2. Of those that a mesh axis runs over, the one named last changes fastest.
Arguments:
- tokens: bfloat16 [4096, 1024], P(('ctx', 'heads')), may hold values from -6 to 6
- d_out: bfloat16 [4096, 1024], P(('ctx', 'heads')), may hold values from -6 to 6
- segment_ids: int32 [4096], P(('ctx', 'heads')), may hold values from 0 to 2, as said below
- position_ids: int32 [4096], P(('ctx', 'heads')), may hold values from 0 to 2047, as said below
- w_qkv: bfloat16 [1024, 3072], P('ctx'), may hold values from -0.1875 to 0.1875
- w_attn: bfloat16 [1024, 1024], P('ctx'), may hold values from -1.5 to 1.5
- w_in: bfloat16 [1024, 5248], P('ctx'), may hold values from -0.1875 to 0.1875
- w_out: bfloat16 [2624, 1024], P(None, 'ctx'), may hold values from -0.25 to 0.25
- gain_attn: bfloat16 [1024], P('ctx'), may hold values from 0.25 to 1.75
- gain_mlp: bfloat16 [1024], P('ctx'), may hold values from 0.25 to 1.75
Outputs:
- out: bfloat16 [4096, 1024], P(('ctx', 'heads'))
- grad_input: float32 [4096, 1024], P(('ctx', 'heads'))
- grad_w_qkv: float32 [1024, 3072], P('ctx')
- grad_w_attn: float32 [1024, 1024], P('ctx')
- grad_w_in: float32 [1024, 5248], P('ctx')
- grad_w_out: float32 [2624, 1024], P(None, 'ctx')
- grad_gain_attn: float32 [1024], P('ctx')
- grad_gain_mlp: float32 [1024], P('ctx')
The draws below stay inside these ranges and needn't reach their ends.
Inputs may be any that keep to these rules, and one draw needn't show every extreme that they name: `segment_ids`: starts at 0 and rises by 0 or 1 from one token to the next. The tokens fall into aligned blocks of 2048; one block, at a drawn place, is one sequence of exactly 2048 tokens, every other block holds two sequences split at a drawn point, each of 512 tokens or more. `position_ids`: the number of earlier tokens with the same segment id.
All inputs are finite; a program needn't handle non-finite values.
Results may differ from the reference program's by a relative error of at most 0.02.
Values may be sent and summed in bfloat16 or wider, within the bound.
A program may use at most 192 MiB of HBM per device.

```python
import jax
import jax.numpy as jnp
from jax import lax

D = 1024
H = 16
HD = 64
FF = 2624
TOK_DEV = 128
SEQ_MAX = 2048
TOKENS = 4096
N_HEADS = 4


def segment_layout(key):
    folded = jax.random.fold_in(key, 11)
    cut_key, pick_key = jax.random.split(folded)
    block_total = TOKENS // SEQ_MAX
    cuts = jax.random.randint(cut_key, (block_total,), SEQ_MAX // 4, 3 * SEQ_MAX // 4 + 1).astype(jnp.int32)
    whole_block = jax.random.randint(pick_key, (), 0, block_total).astype(jnp.int32)
    places = jnp.arange(TOKENS, dtype=jnp.int32)
    block_of = (places // SEQ_MAX).astype(jnp.int32)
    within = (places % SEQ_MAX).astype(jnp.int32)
    block_cut = jnp.take(cuts, block_of)
    second = jnp.logical_and(within >= block_cut, block_of != whole_block).astype(jnp.int32)
    later = (block_of > whole_block).astype(jnp.int32)
    ids = 2 * block_of - later + second
    positions = within - second * block_cut
    return (ids.astype(jnp.int32), positions.astype(jnp.int32))


def draw_segment_ids(key, part):
    return segment_layout(key)[0]


def draw_position_ids(key, part):
    return segment_layout(key)[1]


def level_of(rng, shape, shards, least, top_value):
    gain, own = 1.0, jax.random.fold_in(rng, 6)
    for axis_at, parts in shards:
        heights = jnp.exp(jax.random.uniform(jax.random.fold_in(own, axis_at), (parts,), jnp.float32, least / len(shards), top_value / len(shards)))
        gain = gain * jnp.repeat(heights, shape[axis_at] // parts).reshape([-1 if axis == axis_at else 1 for axis in range(len(shape))])
    return gain


def noise(rng, extent, width, limit, cuts=(), held_as=jnp.bfloat16):
    factor_of = level_of(rng, extent, cuts, -0.22, 0.18) if cuts else 1.0
    entries = jax.random.normal(rng, extent, jnp.float32) * width * factor_of
    return jnp.minimum(jnp.maximum(entries, -limit), limit).astype(held_as)


def setup_inputs(seed: int = 0) -> dict:
    key_of = jax.random.split(jax.random.key(seed), 11)
    return {
        "tokens": noise(key_of[0], (TOKENS, D), 1.0, 6.0, ((0, 32),)),
        "d_out": noise(key_of[1], (TOKENS, D), 1.0, 6.0, ((0, 32),)),
        "segment_ids": draw_segment_ids(jax.random.fold_in(key_of[10], 71), 0),
        "position_ids": draw_position_ids(jax.random.fold_in(key_of[10], 71), 0),
        "w_qkv": noise(key_of[4], (D, 3 * D), D ** -0.5, 0.1875, ((0, 8),)),
        "w_attn": noise(key_of[5], (D, D), (D // 64) ** -0.5, 1.5, ((0, 8),)),
        "w_in": noise(key_of[6], (D, 2 * FF), D ** -0.5, 0.1875, ((0, 8),)),
        "w_out": noise(key_of[7], (FF, D), (FF // 4) ** -0.5, 0.25, ((1, 8),)),
        "gain_attn": jnp.clip(1.0 + 0.15 * jax.random.normal(key_of[8], (D,), jnp.float32), 0.25, 1.75).astype(jnp.bfloat16),
        "gain_mlp": jnp.clip(1.0 + 0.15 * jax.random.normal(key_of[9], (D,), jnp.float32), 0.25, 1.75).astype(jnp.bfloat16),
    }


@jax.custom_vjp
def low(v):
    return lax.optimization_barrier(v.astype(jnp.bfloat16)).astype(jnp.float32)

@jax.custom_vjp
def low_back(v):
    return v

def low_keep(v):
    return (low(v), None)

def low_pass(kept, grad):
    return (grad,)

def back_keep(v):
    return (v, None)

def back_low(kept, grad):
    return (low(grad),)
low.defvjp(low_keep, low_pass)
low_back.defvjp(back_keep, back_low)

def layer_norm(values, scale_gain):
    average = lax.optimization_barrier(jnp.mean(values, axis=-1, keepdims=True))
    centred = values - average
    inverse_std = lax.rsqrt(lax.optimization_barrier(jnp.mean(centred * centred, axis=-1, keepdims=True)) + 1e-05)
    return centred * inverse_std * scale_gain

def rope_tables(positions, head_dim):
    half_dim = head_dim // 2
    freqs = jnp.power(160000.0, -(2.0 * jnp.arange(half_dim, dtype=jnp.float32)) / head_dim)
    angles = positions.astype(jnp.float32)[:, None] * freqs[None, :]
    cosine = jnp.concatenate([jnp.cos(angles), jnp.cos(angles)], axis=-1)[:, None, :]
    sine = jnp.concatenate([jnp.sin(angles), jnp.sin(angles)], axis=-1)[:, None, :]
    return (cosine, sine)

def rotate(values, cosine, sine):
    half_dim = values.shape[-1] // 2
    turned = jnp.concatenate([-values[..., half_dim:], values[..., :half_dim]], axis=-1)
    return values * cosine + turned * sine

def attention(queries, keys, values, segments):
    block_rows = TOK_DEV * N_HEADS
    window = min(block_rows + 2 * SEQ_MAX, TOKENS)
    highest = lax.Precision.HIGHEST

    def one_block(block_index):
        start = (block_index * block_rows).astype(jnp.int32)
        key_start = jnp.clip(start - SEQ_MAX, 0, TOKENS - window).astype(jnp.int32)
        query_block = lax.dynamic_slice_in_dim(queries, start, block_rows, 0)
        query_marks = lax.dynamic_slice_in_dim(segments, start, block_rows, 0)
        key_block = lax.dynamic_slice_in_dim(keys, key_start, window, 0)
        value_block = lax.dynamic_slice_in_dim(values, key_start, window, 0)
        key_marks = lax.dynamic_slice_in_dim(segments, key_start, window, 0)
        raw = jnp.einsum('qhd,khd->hqk', query_block, key_block, precision=highest) * 0.125
        allowed = (query_marks[:, None] == key_marks[None, :])[None]
        scores = low_back(jnp.where(allowed, raw, -1e+30))
        shifted = jnp.exp(scores - lax.optimization_barrier(jnp.max(scores, axis=-1, keepdims=True)))
        probability = shifted / lax.optimization_barrier(jnp.sum(shifted, axis=-1, keepdims=True))
        mixed = jnp.einsum('hqk,khd->qhd', low(probability), value_block, precision=highest)
        return mixed.reshape(block_rows, H * HD)
    blocks = lax.map(jax.checkpoint(one_block), jnp.arange(TOKENS // block_rows, dtype=jnp.int32))
    return blocks.reshape(TOKENS, H * HD)

def reference(tokens, d_out, segment_ids, position_ids, w_qkv, w_attn, w_in, w_out, gain_attn, gain_mlp):
    cosine, sine = rope_tables(position_ids, HD)
    highest = lax.Precision.HIGHEST

    def forward(residual_in, mat_qkv, mat_attn, mat_in, mat_out, gain_one, gain_two):
        attn_input = low(layer_norm(residual_in, gain_one))
        projected = low_back(jnp.dot(attn_input, mat_qkv, precision=highest)).reshape(TOKENS, 3, H, HD)
        queries = low_back(low(rotate(projected[:, 0], cosine, sine)))
        keys = low_back(low(rotate(projected[:, 1], cosine, sine)))
        values = low_back(low(projected[:, 2]))
        attended = low_back(low(attention(queries, keys, values, segment_ids)))
        middle = residual_in + low_back(jnp.dot(attended, mat_attn, precision=highest))
        mlp_input = low(layer_norm(middle, gain_two))
        gate_up = low_back(jnp.dot(mlp_input, mat_in, precision=highest))
        mixed = low(jax.nn.gelu(gate_up[:, :FF], approximate=False) * gate_up[:, FF:])
        return middle + low_back(jnp.dot(mixed, mat_out, precision=highest))
    result, pull = jax.vjp(forward, tokens.astype(jnp.float32), w_qkv.astype(jnp.float32), w_attn.astype(jnp.float32), w_in.astype(jnp.float32), w_out.astype(jnp.float32), gain_attn.astype(jnp.float32), gain_mlp.astype(jnp.float32))
    grads = pull(d_out.astype(jnp.float32))
    return (result.astype(jnp.bfloat16), grads[0], grads[1], grads[2], grads[3], grads[4], grads[5], grads[6])
```

```python
import functools

import jax
import jax.numpy as jnp
from jax import lax
from jax.experimental import pallas as pl
from jax.experimental.pallas import tpu as pltpu
from jax.sharding import PartitionSpec as P

H = 16
HD = 64
HALF = HD // 2
FF = 2624
SEQ_MAX = 2048
MASKED = -1e30
MARKS = 16
Q_END = HD
QM_END = Q_END + MARKS
K_END = QM_END + HD
KM_END = K_END + MARKS
V_END = KM_END + HD
BF = jnp.bfloat16
F32 = jnp.float32


def dot(left, right, left_dim, right_dim):
    return lax.dot_general(
        left, right, (((left_dim,), (right_dim,)), ((), ())), preferred_element_type=F32
    )


def norm_parts(values):
    average = jnp.mean(values, axis=-1, keepdims=True)
    centred = values - average
    inverse_std = lax.rsqrt(jnp.mean(centred * centred, axis=-1, keepdims=True) + 1e-05)
    return centred * inverse_std, inverse_std


def norm_back(upstream, normed, inverse_std, gain):
    scaled = upstream * gain
    return inverse_std * (
        scaled
        - jnp.mean(scaled, axis=-1, keepdims=True)
        - normed * jnp.mean(scaled * normed, axis=-1, keepdims=True)
    )


def attend_kernel(tile, qkv_ref, out_ref, wide_ref, lse_ref):
    blocks, _, block = qkv_ref.shape
    per_block = block // tile
    step = pl.program_id(0)
    which = step // per_block
    start = pl.multiple_of(step % per_block * tile, tile)
    query = qkv_ref[which, :QM_END, pl.ds(start, tile)]
    scores = [dot(qkv_ref[j, QM_END:KM_END, :], query, 0, 0) for j in range(blocks)]
    top = functools.reduce(jnp.maximum, [jnp.max(s, axis=0, keepdims=True) for s in scores])
    raised = [jnp.exp(s - top) for s in scores]
    total = functools.reduce(jnp.add, [jnp.sum(e, axis=0, keepdims=True) for e in raised])
    scale = 1.0 / total
    result = jnp.zeros((HD, tile), F32)
    for j in range(blocks):
        result += dot(qkv_ref[j, KM_END:V_END, :], (raised[j] * scale).astype(BF), 1, 0)
    out_ref[which, :, pl.ds(start, tile)] = result.astype(BF)
    wide_ref[which, :, pl.ds(start, tile)] = result
    lse_ref[which, :, pl.ds(start, tile)] = top + jnp.log(total)


def attend(qkv, tile):
    blocks, _, block = qkv.shape
    whole = lambda rows: pl.BlockSpec((blocks, rows, block), lambda i: (0, 0, 0))
    count = blocks * block
    return pl.pallas_call(
        functools.partial(attend_kernel, tile),
        grid=(count // tile,),
        in_specs=[whole(V_END)],
        out_specs=[whole(HD), whole(HD), whole(1)],
        out_shape=[
            jax.ShapeDtypeStruct((blocks, HD, block), BF),
            jax.ShapeDtypeStruct((blocks, HD, block), F32),
            jax.ShapeDtypeStruct((blocks, 1, block), F32),
        ],
        compiler_params=pltpu.CompilerParams(vmem_limit_bytes=40 << 20),
        cost_estimate=pl.CostEstimate(
            flops=count * count * HD * 8, bytes_accessed=count * 1024, transcendentals=count * count
        ),
        name="attend",
    )(qkv)


def attend_back_kernel(tile, qkv_ref, grad_ref, wide_ref, lse_ref, out_ref, sums):
    blocks, _, block = qkv_ref.shape
    per_block = block // tile
    step = pl.program_id(0)

    @pl.when(step == 0)
    def _():
        sums[...] = jnp.zeros_like(sums)

    which = step // per_block
    start = pl.multiple_of(step % per_block * tile, tile)
    query = qkv_ref[which, :QM_END, pl.ds(start, tile)]
    grad = grad_ref[which, :, pl.ds(start, tile)]
    delta = jnp.sum(
        grad.astype(F32) * wide_ref[which, :, pl.ds(start, tile)], axis=0, keepdims=True
    )
    lse = lse_ref[which, :, pl.ds(start, tile)]
    grad_query = jnp.zeros((HD, tile), F32)
    for j in range(blocks):
        prob = jnp.exp(dot(qkv_ref[j, QM_END:KM_END, :], query, 0, 0) - lse)
        grad_prob = dot(qkv_ref[j, KM_END:V_END, :], grad, 0, 0)
        grad_score = (prob * (grad_prob - delta)).astype(BF)
        grad_query += dot(qkv_ref[j, QM_END:K_END, :], grad_score, 1, 0)
        sums[j, :HD, :] += dot(query[:HD], grad_score, 1, 1)
        sums[j, HD:, :] += dot(grad, prob.astype(BF), 1, 1)
    out_ref[which, :HD, pl.ds(start, tile)] = (grad_query * 0.125).astype(BF)

    @pl.when(step == pl.num_programs(0) - 1)
    def _():
        out_ref[:, HD:, :] = sums[...].astype(BF)


def attend_back(qkv, grad, wide, lse, tile):
    blocks, _, block = qkv.shape
    whole = lambda rows: pl.BlockSpec((blocks, rows, block), lambda i: (0, 0, 0))
    count = blocks * block
    return pl.pallas_call(
        functools.partial(attend_back_kernel, tile),
        grid=(count // tile,),
        in_specs=[whole(V_END), whole(HD), whole(HD), whole(1)],
        out_specs=whole(3 * HD),
        out_shape=jax.ShapeDtypeStruct((blocks, 3 * HD, block), BF),
        scratch_shapes=[pltpu.VMEM((blocks, 2 * HD, block), F32)],
        compiler_params=pltpu.CompilerParams(vmem_limit_bytes=40 << 20),
        cost_estimate=pl.CostEstimate(
            flops=count * count * HD * 20, bytes_accessed=count * 1536, transcendentals=count * count
        ),
        name="attend_back",
    )(qkv, grad, wide, lse)


def body(tokens, d_out, segment_ids, position_ids, w_qkv, w_attn, w_in, w_out, gain_attn, gain_mlp):
    groups = lax.axis_size("heads")
    ctx_count = lax.axis_size("ctx")
    member = lax.axis_index("heads")
    rows, width = tokens.shape
    shard = w_qkv.shape[0]
    block = rows * groups
    reach = SEQ_MAX // block
    per_group = H // groups
    assert per_group == reach
    lanes = per_group * HD
    hidden = FF // groups
    padded = -(-hidden // 128) * 128
    tile = min(512, block)
    teams = [[reach * i + j for j in range(reach)] for i in range(ctx_count // reach)]

    def swap(value):
        return lax.all_to_all(
            value, "ctx", split_axis=0, concat_axis=0, axis_index_groups=teams, tiled=True
        )

    def own_rows(value):
        return lax.dynamic_slice_in_dim(value, member * rows, rows, 0)

    def heads_sum(value):
        parts = lax.all_to_all(
            value.astype(BF).reshape(groups, rows, width),
            "heads",
            split_axis=0,
            concat_axis=0,
            tiled=True,
        )
        return jnp.sum(parts.astype(F32), axis=0)

    extra = jnp.stack([position_ids // 256, position_ids % 256, segment_ids % 2], axis=1)
    extra = jnp.pad(extra.astype(BF), ((0, 0), (0, 125)))
    gathered_block = lax.all_gather(
        jnp.concatenate([tokens, d_out, extra], axis=1), "heads", axis=0, tiled=True
    )
    qkv_part = lax.dynamic_slice_in_dim(
        w_qkv.reshape(shard, 3, width), member * lanes, lanes, 2
    ).reshape(shard, 3 * lanes)
    gains = jnp.pad(jnp.stack([gain_attn, gain_mlp], axis=1), ((0, 0), (0, 126)))
    first_weights = lax.all_gather(
        jnp.concatenate([qkv_part, gains], axis=1), "ctx", axis=0, tiled=True
    )

    def fit(value):
        return jnp.pad(value, ((0, 0), (0, padded - hidden)))

    left_part = fit(lax.dynamic_slice_in_dim(w_in, member * hidden, hidden, 1))
    right_part = fit(lax.dynamic_slice_in_dim(w_in, FF + member * hidden, hidden, 1))
    out_part = fit(lax.dynamic_slice_in_dim(w_out, member * hidden, hidden, 0).T)
    full_attn = lax.all_gather(w_attn, "ctx", axis=0, tiled=True)
    mlp_weights = lax.all_gather(
        jnp.concatenate([left_part, right_part, out_part], axis=1), "ctx", axis=0, tiled=True
    )
    in_weights = mlp_weights[:, : 2 * padded]
    out_weights = mlp_weights[:, 2 * padded :]

    residual_in = gathered_block[:, :width].astype(F32)
    upstream = gathered_block[:, width : 2 * width]
    digits = gathered_block[:, 2 * width :].astype(F32)
    positions = digits[:, 0] * 256.0 + digits[:, 1]
    parity = digits[:, 2][None, :]
    freqs = jnp.power(160000.0, -(2.0 * jnp.arange(HALF, dtype=F32)) / HD)
    angles = freqs[:, None] * positions[None, :]
    cosine = jnp.cos(angles)
    sine = jnp.sin(angles)

    qkv_weights = first_weights[:, : 3 * lanes]
    gain_one = first_weights[:, 3 * lanes].astype(F32)
    gain_two = first_weights[:, 3 * lanes + 1].astype(F32)
    plain_one, inverse_one = norm_parts(residual_in)
    attn_input = (plain_one * gain_one).astype(BF)
    projected = dot(qkv_weights, attn_input, 0, 1).reshape(3, per_group, 2, HALF, block)

    def turn(value):
        front, back = value[:, 0], value[:, 1]
        return jnp.concatenate([front * cosine - back * sine, back * cosine + front * sine], axis=1)

    def mark_rows(first, second):
        pad = jnp.zeros((MARKS - 2, block), F32)
        stacked = jnp.concatenate([first, second, pad], axis=0)
        return jnp.broadcast_to(stacked[None], (per_group, MARKS, block))

    outgoing = jnp.concatenate(
        [
            turn(projected[0]) * 0.125,
            mark_rows(parity, 1.0 - parity),
            turn(projected[1]),
            mark_rows((1.0 - parity) * MASKED, parity * MASKED),
            projected[2].reshape(per_group, HD, block),
        ],
        axis=1,
    ).astype(BF)
    qkv = swap(outgoing)
    attended, attended_wide, lse = attend(qkv, tile)
    returned = swap(attended).reshape(lanes, block)
    attended_all = lax.all_gather(returned, "heads", axis=0, tiled=True)
    middle = residual_in + dot(attended_all, full_attn, 0, 0)
    plain_two, inverse_two = norm_parts(middle)
    mlp_input = (plain_two * gain_two).astype(BF)
    gate_up = dot(mlp_input, in_weights, 1, 0)
    gate_left = gate_up[:, :padded]
    gate_right = gate_up[:, padded:]
    normal_cdf = 0.5 * (1.0 + lax.erf(gate_left * 0.7071067811865476))
    gelu = gate_left * normal_cdf
    density = jnp.exp(-0.5 * gate_left * gate_left) * 0.3989422804014327
    mixed = (gelu * gate_right).astype(BF)
    grad_mixed = dot(upstream, out_weights, 1, 0)
    grad_left = grad_mixed * gate_right * (normal_cdf + gate_left * density)
    grad_gate_up = jnp.concatenate([grad_left, grad_mixed * gelu], axis=1).astype(BF)
    grad_mlp_part = dot(grad_gate_up, in_weights, 1, 1)
    grad_gain_two = jnp.sum(grad_mlp_part * plain_two, axis=0)
    grad_norm_mid = norm_back(
        heads_sum(grad_mlp_part), own_rows(plain_two), own_rows(inverse_two), gain_two
    )
    grad_middle = d_out.astype(F32) + grad_norm_mid
    grad_branch = lax.all_gather(grad_middle.astype(BF), "heads", axis=0, tiled=True)
    attn_rows = lax.dynamic_slice_in_dim(full_attn, member * lanes, lanes, 0)
    grad_attended = dot(attn_rows, grad_branch, 1, 1).astype(BF).reshape(per_group, HD, block)
    grad_heads = swap(grad_attended)
    result = (own_rows(middle) + heads_sum(dot(mixed, out_weights, 1, 1))).astype(BF)
    grad_out_part = dot(upstream, mixed, 0, 0)
    grad_in_part = dot(mlp_input, grad_gate_up, 0, 0)
    branch_columns = lax.dynamic_slice_in_dim(grad_branch, member * lanes, lanes, 1)
    grad_attn_part = dot(attended_all, branch_columns, 1, 0)
    late = lax.psum_scatter(
        jnp.concatenate([grad_in_part, grad_out_part, grad_attn_part], axis=1).astype(BF),
        "ctx",
        scatter_dimension=0,
        tiled=True,
    )
    grad_qkv = swap(attend_back(qkv, grad_heads, attended_wide, lse, tile))
    grad_qkv = grad_qkv.astype(F32).reshape(per_group, 3, 2, HALF, block)

    def turn_back(value):
        front, back = value[:, 0], value[:, 1]
        return jnp.stack([front * cosine + back * sine, back * cosine - front * sine], axis=1)

    grad_projected = (
        jnp.stack([turn_back(grad_qkv[:, 0]), turn_back(grad_qkv[:, 1]), grad_qkv[:, 2]])
        .reshape(3 * lanes, block)
        .astype(BF)
    )
    grad_attn_in = dot(grad_projected, qkv_weights, 0, 1)
    grad_gain_one = jnp.sum(grad_attn_in * plain_one, axis=0)
    grad_qkv_part = dot(attn_input, grad_projected, 0, 1)
    grad_gains = jnp.pad(jnp.stack([grad_gain_one, grad_gain_two], axis=1), ((0, 0), (0, 126)))
    last = lax.psum_scatter(
        jnp.concatenate([grad_qkv_part, grad_gains], axis=1).astype(BF),
        "ctx",
        scatter_dimension=0,
        tiled=True,
    )
    grad_input = grad_middle + norm_back(
        heads_sum(grad_attn_in), own_rows(plain_one), own_rows(inverse_one), gain_one
    )
    late_all = lax.all_gather(late, "heads", axis=0)
    last_all = lax.all_gather(last, "heads", axis=0)
    sum_qkv = (
        last_all[:, :, : 3 * lanes]
        .reshape(groups, shard, 3, lanes)
        .transpose(1, 2, 0, 3)
        .reshape(shard, 3 * width)
        .astype(F32)
    )
    gain_sums = jnp.sum(last_all[:, :, 3 * lanes : 3 * lanes + 2].astype(F32), axis=0)

    def columns(start, size):
        piece = late_all[:, :, start : start + size]
        return piece.transpose(1, 0, 2).reshape(shard, groups * size).astype(F32)

    sum_in = jnp.concatenate([columns(0, hidden), columns(padded, hidden)], axis=1)
    sum_out = (
        late_all[:, :, 2 * padded : 2 * padded + hidden]
        .transpose(0, 2, 1)
        .reshape(groups * hidden, shard)
        .astype(F32)
    )
    sum_attn = columns(3 * padded, lanes)
    return (
        result,
        grad_input,
        sum_qkv,
        sum_attn,
        sum_in,
        sum_out,
        gain_sums[:, 0],
        gain_sums[:, 1],
    )


def solution(mesh):
    return jax.shard_map(
        body,
        mesh=mesh,
        in_specs=(
            P(("ctx", "heads"), None),
            P(("ctx", "heads"), None),
            P(("ctx", "heads")),
            P(("ctx", "heads")),
            P("ctx", None),
            P("ctx", None),
            P("ctx", None),
            P(None, "ctx"),
            P("ctx"),
            P("ctx"),
        ),
        out_specs=(
            P(("ctx", "heads"), None),
            P(("ctx", "heads"), None),
            P("ctx", None),
            P("ctx", None),
            P("ctx", None),
            P(None, "ctx"),
            P("ctx"),
            P("ctx"),
        ),
        check_vma=False,
    )
```

```python
import functools

import jax
import jax.numpy as jnp
from jax import lax
from jax.experimental import pallas as pl
from jax.experimental.pallas import tpu as pltpu
from jax.sharding import PartitionSpec as P

H = 16
HD = 64
HALF = HD // 2
FF = 2624
SEQ_MAX = 2048
MASKED = -1e30
MARKS = 16
Q_END = HD
QM_END = Q_END + MARKS
K_END = QM_END + HD
KM_END = K_END + MARKS
V_END = KM_END + HD
BF = jnp.bfloat16
F32 = jnp.float32


def dot(left, right, left_dim, right_dim):
    return lax.dot_general(
        left, right, (((left_dim,), (right_dim,)), ((), ())), preferred_element_type=F32
    )


def exchange_kernel(count, axis, split, source, target, send, recv, local):
    place = lax.axis_index(axis)
    base = place // count * count
    me = place - base
    barrier = pltpu.get_barrier_semaphore()
    for step in range(1, count):
        peer = lax.rem(me + step, count)
        pl.semaphore_signal(
            barrier, inc=1, device_id={axis: base + peer}, device_id_type=pl.DeviceIdType.MESH
        )
    pl.semaphore_wait(barrier, count - 1)
    copies = []
    for step in range(1, count):
        peer = lax.rem(me + step, count)
        copy = pltpu.make_async_remote_copy(
            src_ref=source.at[peer] if split else source,
            dst_ref=target.at[me],
            send_sem=send.at[step - 1],
            recv_sem=recv.at[step - 1],
            device_id={axis: base + peer},
            device_id_type=pl.DeviceIdType.MESH,
        )
        copy.start()
        copies.append(copy)
    own = pltpu.make_async_copy(source.at[me] if split else source, target.at[me], local)
    own.start()
    own.wait()
    for copy in copies:
        copy.wait()


def exchange(value, axis, count, split, number):
    shape = value.shape if split else (count, *value.shape)
    moved = value.size * value.dtype.itemsize * (1 if split else count)
    return pl.pallas_call(
        functools.partial(exchange_kernel, count, axis, split),
        in_specs=[pl.BlockSpec(memory_space=pl.ANY)],
        out_specs=pl.BlockSpec(memory_space=pl.ANY),
        out_shape=jax.ShapeDtypeStruct(shape, value.dtype),
        scratch_shapes=[
            pltpu.SemaphoreType.DMA((count - 1,)),
            pltpu.SemaphoreType.DMA((count - 1,)),
            pltpu.SemaphoreType.DMA,
        ],
        compiler_params=pltpu.CompilerParams(collective_id=number, has_side_effects=True),
        cost_estimate=pl.CostEstimate(flops=0, bytes_accessed=moved * 20, transcendentals=0),
        name=f"exchange_{number}",
    )(value)


def norm_parts(values):
    average = jnp.mean(values, axis=-1, keepdims=True)
    centred = values - average
    inverse_std = lax.rsqrt(jnp.mean(centred * centred, axis=-1, keepdims=True) + 1e-05)
    return centred * inverse_std, inverse_std


def norm_back(upstream, normed, inverse_std, gain):
    scaled = upstream * gain
    return inverse_std * (
        scaled
        - jnp.mean(scaled, axis=-1, keepdims=True)
        - normed * jnp.mean(scaled * normed, axis=-1, keepdims=True)
    )


def attend_kernel(tile, qkv_ref, out_ref, wide_ref, lse_ref):
    blocks, _, block = qkv_ref.shape
    per_block = block // tile
    step = pl.program_id(0)
    which = step // per_block
    start = pl.multiple_of(step % per_block * tile, tile)
    query = qkv_ref[which, :QM_END, pl.ds(start, tile)]
    scores = [dot(qkv_ref[j, QM_END:KM_END, :], query, 0, 0) for j in range(blocks)]
    top = functools.reduce(jnp.maximum, [jnp.max(s, axis=0, keepdims=True) for s in scores])
    raised = [jnp.exp(s - top) for s in scores]
    total = functools.reduce(jnp.add, [jnp.sum(e, axis=0, keepdims=True) for e in raised])
    scale = 1.0 / total
    result = jnp.zeros((HD, tile), F32)
    for j in range(blocks):
        result += dot(qkv_ref[j, KM_END:V_END, :], (raised[j] * scale).astype(BF), 1, 0)
    out_ref[which, :, pl.ds(start, tile)] = result.astype(BF)
    wide_ref[which, :, pl.ds(start, tile)] = result
    lse_ref[which, :, pl.ds(start, tile)] = top + jnp.log(total)


def attend(qkv, tile):
    blocks, _, block = qkv.shape
    whole = lambda rows: pl.BlockSpec((blocks, rows, block), lambda i: (0, 0, 0))
    count = blocks * block
    return pl.pallas_call(
        functools.partial(attend_kernel, tile),
        grid=(count // tile,),
        in_specs=[whole(V_END)],
        out_specs=[whole(HD), whole(HD), whole(1)],
        out_shape=[
            jax.ShapeDtypeStruct((blocks, HD, block), BF),
            jax.ShapeDtypeStruct((blocks, HD, block), F32),
            jax.ShapeDtypeStruct((blocks, 1, block), F32),
        ],
        compiler_params=pltpu.CompilerParams(vmem_limit_bytes=40 << 20),
        cost_estimate=pl.CostEstimate(
            flops=count * count * HD * 8, bytes_accessed=count * 1024, transcendentals=count * count
        ),
        name="attend",
    )(qkv)


def attend_back_kernel(tile, qkv_ref, grad_ref, wide_ref, lse_ref, out_ref, sums):
    blocks, _, block = qkv_ref.shape
    per_block = block // tile
    step = pl.program_id(0)

    @pl.when(step == 0)
    def _():
        sums[...] = jnp.zeros_like(sums)

    which = step // per_block
    start = pl.multiple_of(step % per_block * tile, tile)
    query = qkv_ref[which, :QM_END, pl.ds(start, tile)]
    grad = grad_ref[which, :, pl.ds(start, tile)]
    delta = jnp.sum(
        grad.astype(F32) * wide_ref[which, :, pl.ds(start, tile)], axis=0, keepdims=True
    )
    lse = lse_ref[which, :, pl.ds(start, tile)]
    grad_query = jnp.zeros((HD, tile), F32)
    for j in range(blocks):
        prob = jnp.exp(dot(qkv_ref[j, QM_END:KM_END, :], query, 0, 0) - lse)
        grad_prob = dot(qkv_ref[j, KM_END:V_END, :], grad, 0, 0)
        grad_score = (prob * (grad_prob - delta)).astype(BF)
        grad_query += dot(qkv_ref[j, QM_END:K_END, :], grad_score, 1, 0)
        sums[j, :HD, :] += dot(query[:HD], grad_score, 1, 1)
        sums[j, HD:, :] += dot(grad, prob.astype(BF), 1, 1)
    out_ref[which, :HD, pl.ds(start, tile)] = (grad_query * 0.125).astype(BF)

    @pl.when(step == pl.num_programs(0) - 1)
    def _():
        out_ref[:, HD:, :] = sums[...].astype(BF)


def attend_back(qkv, grad, wide, lse, tile):
    blocks, _, block = qkv.shape
    whole = lambda rows: pl.BlockSpec((blocks, rows, block), lambda i: (0, 0, 0))
    count = blocks * block
    return pl.pallas_call(
        functools.partial(attend_back_kernel, tile),
        grid=(count // tile,),
        in_specs=[whole(V_END), whole(HD), whole(HD), whole(1)],
        out_specs=whole(3 * HD),
        out_shape=jax.ShapeDtypeStruct((blocks, 3 * HD, block), BF),
        scratch_shapes=[pltpu.VMEM((blocks, 2 * HD, block), F32)],
        compiler_params=pltpu.CompilerParams(vmem_limit_bytes=40 << 20),
        cost_estimate=pl.CostEstimate(
            flops=count * count * HD * 20, bytes_accessed=count * 1536, transcendentals=count * count
        ),
        name="attend_back",
    )(qkv, grad, wide, lse)


def body(tokens, d_out, segment_ids, position_ids, w_qkv, w_attn, w_in, w_out, gain_attn, gain_mlp):
    groups = lax.axis_size("heads")
    member = lax.axis_index("heads")
    rows, width = tokens.shape
    shard = w_qkv.shape[0]
    block = rows * groups
    reach = SEQ_MAX // block
    per_group = H // groups
    assert per_group == reach
    lanes = per_group * HD
    hidden = FF // groups
    padded = -(-hidden // 128) * 128
    tile = min(512, block)

    def swap(value, number):
        return exchange(value, "ctx", reach, True, number)

    def heads_gather(value, number):
        return exchange(value, "heads", groups, False, number)

    def own_rows(value):
        return lax.dynamic_slice_in_dim(value, member * rows, rows, 0)

    def heads_sum(value, number):
        parts = exchange(
            value.astype(BF).reshape(groups, rows, width), "heads", groups, True, number
        )
        return jnp.sum(parts.astype(F32), axis=0)

    extra = jnp.stack([position_ids // 256, position_ids % 256, segment_ids % 2], axis=1)
    extra = jnp.pad(extra.astype(BF), ((0, 0), (0, 125)))
    gathered_block = heads_gather(jnp.concatenate([tokens, d_out, extra], axis=1), 0).reshape(
        block, 2 * width + 128
    )
    qkv_part = lax.dynamic_slice_in_dim(
        w_qkv.reshape(shard, 3, width), member * lanes, lanes, 2
    ).reshape(shard, 3 * lanes)
    gains = jnp.pad(jnp.stack([gain_attn, gain_mlp], axis=1), ((0, 0), (0, 126)))
    first_weights = lax.all_gather(
        jnp.concatenate([qkv_part, gains], axis=1), "ctx", axis=0, tiled=True
    )

    def fit(value):
        return jnp.pad(value, ((0, 0), (0, padded - hidden)))

    left_part = fit(lax.dynamic_slice_in_dim(w_in, member * hidden, hidden, 1))
    right_part = fit(lax.dynamic_slice_in_dim(w_in, FF + member * hidden, hidden, 1))
    out_part = fit(lax.dynamic_slice_in_dim(w_out, member * hidden, hidden, 0).T)
    full_attn = lax.all_gather(w_attn, "ctx", axis=0, tiled=True)
    mlp_weights = lax.all_gather(
        jnp.concatenate([left_part, right_part, out_part], axis=1), "ctx", axis=0, tiled=True
    )
    in_weights = mlp_weights[:, : 2 * padded]
    out_weights = mlp_weights[:, 2 * padded :]

    residual_in = gathered_block[:, :width].astype(F32)
    upstream = gathered_block[:, width : 2 * width]
    digits = gathered_block[:, 2 * width :].astype(F32)
    positions = digits[:, 0] * 256.0 + digits[:, 1]
    parity = digits[:, 2][None, :]
    freqs = jnp.power(160000.0, -(2.0 * jnp.arange(HALF, dtype=F32)) / HD)
    angles = freqs[:, None] * positions[None, :]
    cosine = jnp.cos(angles)
    sine = jnp.sin(angles)

    qkv_weights = first_weights[:, : 3 * lanes]
    gain_one = first_weights[:, 3 * lanes].astype(F32)
    gain_two = first_weights[:, 3 * lanes + 1].astype(F32)
    plain_one, inverse_one = norm_parts(residual_in)
    attn_input = (plain_one * gain_one).astype(BF)
    projected = dot(qkv_weights, attn_input, 0, 1).reshape(3, per_group, 2, HALF, block)

    def turn(value):
        front, back = value[:, 0], value[:, 1]
        return jnp.concatenate([front * cosine - back * sine, back * cosine + front * sine], axis=1)

    def mark_rows(first, second):
        pad = jnp.zeros((MARKS - 2, block), F32)
        stacked = jnp.concatenate([first, second, pad], axis=0)
        return jnp.broadcast_to(stacked[None], (per_group, MARKS, block))

    outgoing = jnp.concatenate(
        [
            turn(projected[0]) * 0.125,
            mark_rows(parity, 1.0 - parity),
            turn(projected[1]),
            mark_rows((1.0 - parity) * MASKED, parity * MASKED),
            projected[2].reshape(per_group, HD, block),
        ],
        axis=1,
    ).astype(BF)
    qkv = swap(outgoing, 1)
    attended, attended_wide, lse = attend(qkv, tile)
    returned = swap(attended, 2).reshape(lanes, block)
    attended_all = heads_gather(returned, 3).reshape(width, block)
    middle = residual_in + dot(attended_all, full_attn, 0, 0)
    plain_two, inverse_two = norm_parts(middle)
    mlp_input = (plain_two * gain_two).astype(BF)
    gate_up = dot(mlp_input, in_weights, 1, 0)
    gate_left = gate_up[:, :padded]
    gate_right = gate_up[:, padded:]
    normal_cdf = 0.5 * (1.0 + lax.erf(gate_left * 0.7071067811865476))
    gelu = gate_left * normal_cdf
    density = jnp.exp(-0.5 * gate_left * gate_left) * 0.3989422804014327
    mixed = (gelu * gate_right).astype(BF)
    grad_mixed = dot(upstream, out_weights, 1, 0)
    grad_left = grad_mixed * gate_right * (normal_cdf + gate_left * density)
    grad_gate_up = jnp.concatenate([grad_left, grad_mixed * gelu], axis=1).astype(BF)
    grad_out_part = dot(upstream, mixed, 0, 0)
    grad_in_part = dot(mlp_input, grad_gate_up, 0, 0)
    late = lax.psum_scatter(
        jnp.concatenate([grad_in_part, grad_out_part], axis=1).astype(BF),
        "ctx",
        scatter_dimension=0,
        tiled=True,
    )
    grad_mlp_part = dot(grad_gate_up, in_weights, 1, 1)
    grad_gain_two = jnp.sum(grad_mlp_part * plain_two, axis=0)
    grad_norm_mid = norm_back(
        heads_sum(grad_mlp_part, 4), own_rows(plain_two), own_rows(inverse_two), gain_two
    )
    grad_middle = d_out.astype(F32) + grad_norm_mid
    grad_branch = heads_gather(grad_middle.astype(BF), 5).reshape(block, width)
    attn_rows = lax.dynamic_slice_in_dim(full_attn, member * lanes, lanes, 0)
    grad_attended = dot(attn_rows, grad_branch, 1, 1).astype(BF).reshape(per_group, HD, block)
    grad_heads = swap(grad_attended, 6)
    branch_columns = lax.dynamic_slice_in_dim(grad_branch, member * lanes, lanes, 1)
    grad_attn_part = dot(attended_all, branch_columns, 1, 0)
    grad_qkv = swap(attend_back(qkv, grad_heads, attended_wide, lse, tile), 7)
    grad_qkv = grad_qkv.astype(F32).reshape(per_group, 3, 2, HALF, block)

    def turn_back(value):
        front, back = value[:, 0], value[:, 1]
        return jnp.stack([front * cosine + back * sine, back * cosine - front * sine], axis=1)

    grad_projected = (
        jnp.stack([turn_back(grad_qkv[:, 0]), turn_back(grad_qkv[:, 1]), grad_qkv[:, 2]])
        .reshape(3 * lanes, block)
        .astype(BF)
    )
    grad_attn_in = dot(grad_projected, qkv_weights, 0, 1)
    grad_gain_one = jnp.sum(grad_attn_in * plain_one, axis=0)
    grad_qkv_part = dot(attn_input, grad_projected, 0, 1)
    grad_gains = jnp.pad(jnp.stack([grad_gain_one, grad_gain_two], axis=1), ((0, 0), (0, 126)))
    last = lax.psum_scatter(
        jnp.concatenate([grad_qkv_part, grad_gains, grad_attn_part], axis=1).astype(BF),
        "ctx",
        scatter_dimension=0,
        tiled=True,
    )
    grad_input = grad_middle + norm_back(
        heads_sum(grad_attn_in, 8), own_rows(plain_one), own_rows(inverse_one), gain_one
    )
    mixed, _ = lax.optimization_barrier((mixed, grad_input))
    result = (own_rows(middle) + heads_sum(dot(mixed, out_weights, 1, 1), 9)).astype(BF)
    late_all = heads_gather(late, 10)
    last_all = heads_gather(last, 11)
    sum_qkv = (
        last_all[:, :, : 3 * lanes]
        .reshape(groups, shard, 3, lanes)
        .transpose(1, 2, 0, 3)
        .reshape(shard, 3 * width)
        .astype(F32)
    )
    gain_sums = jnp.sum(last_all[:, :, 3 * lanes : 3 * lanes + 2].astype(F32), axis=0)

    def columns(start, size, held=late_all):
        piece = held[:, :, start : start + size]
        return piece.transpose(1, 0, 2).reshape(shard, groups * size).astype(F32)

    sum_in = jnp.concatenate([columns(0, hidden), columns(padded, hidden)], axis=1)
    sum_out = (
        late_all[:, :, 2 * padded : 2 * padded + hidden]
        .transpose(0, 2, 1)
        .reshape(groups * hidden, shard)
        .astype(F32)
    )
    sum_attn = columns(3 * lanes + 128, lanes, last_all)
    return (
        result,
        grad_input,
        sum_qkv,
        sum_attn,
        sum_in,
        sum_out,
        gain_sums[:, 0],
        gain_sums[:, 1],
    )


def solution(mesh):
    return jax.shard_map(
        body,
        mesh=mesh,
        in_specs=(
            P(("ctx", "heads"), None),
            P(("ctx", "heads"), None),
            P(("ctx", "heads")),
            P(("ctx", "heads")),
            P("ctx", None),
            P("ctx", None),
            P("ctx", None),
            P(None, "ctx"),
            P("ctx"),
            P("ctx"),
        ),
        out_specs=(
            P(("ctx", "heads"), None),
            P(("ctx", "heads"), None),
            P("ctx", None),
            P("ctx", None),
            P("ctx", None),
            P(None, "ctx"),
            P("ctx"),
            P("ctx"),
        ),
        check_vma=False,
    )
```

```python
import functools

import jax
import jax.numpy as jnp
from jax import lax
from jax.experimental import pallas as pl
from jax.experimental.pallas import tpu as pltpu
from jax.sharding import PartitionSpec as P

H = 16
HD = 64
HALF = HD // 2
FF = 2624
SEQ_MAX = 2048
MASKED = -1e30
MARKS = 16
Q_END = HD
QM_END = Q_END + MARKS
K_END = QM_END + HD
KM_END = K_END + MARKS
V_END = KM_END + HD
BF = jnp.bfloat16
F32 = jnp.float32


def dot(left, right, left_dim, right_dim):
    return lax.dot_general(
        left, right, (((left_dim,), (right_dim,)), ((), ())), preferred_element_type=F32
    )


def exchange_kernel(count, axis, split, source, target, send, recv, local):
    place = lax.axis_index(axis)
    base = place // count * count
    me = place - base
    barrier = pltpu.get_barrier_semaphore()
    for step in range(1, count):
        peer = lax.rem(me + step, count)
        pl.semaphore_signal(
            barrier, inc=1, device_id={axis: base + peer}, device_id_type=pl.DeviceIdType.MESH
        )
    pl.semaphore_wait(barrier, count - 1)
    copies = []
    for step in range(1, count):
        peer = lax.rem(me + step, count)
        copy = pltpu.make_async_remote_copy(
            src_ref=source.at[peer] if split else source,
            dst_ref=target.at[me],
            send_sem=send.at[step - 1],
            recv_sem=recv.at[step - 1],
            device_id={axis: base + peer},
            device_id_type=pl.DeviceIdType.MESH,
        )
        copy.start()
        copies.append(copy)
    own = pltpu.make_async_copy(source.at[me] if split else source, target.at[me], local)
    own.start()
    own.wait()
    for copy in copies:
        copy.wait()


def exchange(value, axis, count, split, number):
    shape = value.shape if split else (count, *value.shape)
    moved = value.size * value.dtype.itemsize * (1 if split else count)
    return pl.pallas_call(
        functools.partial(exchange_kernel, count, axis, split),
        in_specs=[pl.BlockSpec(memory_space=pl.ANY)],
        out_specs=pl.BlockSpec(memory_space=pl.ANY),
        out_shape=jax.ShapeDtypeStruct(shape, value.dtype),
        scratch_shapes=[
            pltpu.SemaphoreType.DMA((count - 1,)),
            pltpu.SemaphoreType.DMA((count - 1,)),
            pltpu.SemaphoreType.DMA,
        ],
        compiler_params=pltpu.CompilerParams(collective_id=number, has_side_effects=True),
        cost_estimate=pl.CostEstimate(flops=0, bytes_accessed=moved, transcendentals=0),
        name=f"exchange_{number}",
    )(value)


def norm_parts(values):
    average = jnp.mean(values, axis=-1, keepdims=True)
    centred = values - average
    inverse_std = lax.rsqrt(jnp.mean(centred * centred, axis=-1, keepdims=True) + 1e-05)
    return centred * inverse_std, inverse_std


def norm_back(upstream, normed, inverse_std, gain):
    scaled = upstream * gain
    return inverse_std * (
        scaled
        - jnp.mean(scaled, axis=-1, keepdims=True)
        - normed * jnp.mean(scaled * normed, axis=-1, keepdims=True)
    )


def attend_kernel(tile, qkv_ref, out_ref, wide_ref, lse_ref):
    blocks, _, block = qkv_ref.shape
    per_block = block // tile
    step = pl.program_id(0)
    which = step // per_block
    start = pl.multiple_of(step % per_block * tile, tile)
    query = qkv_ref[which, :QM_END, pl.ds(start, tile)]
    scores = [dot(qkv_ref[j, QM_END:KM_END, :], query, 0, 0) for j in range(blocks)]
    top = functools.reduce(jnp.maximum, [jnp.max(s, axis=0, keepdims=True) for s in scores])
    raised = [jnp.exp(s - top) for s in scores]
    total = functools.reduce(jnp.add, [jnp.sum(e, axis=0, keepdims=True) for e in raised])
    scale = 1.0 / total
    result = jnp.zeros((HD, tile), F32)
    for j in range(blocks):
        result += dot(qkv_ref[j, KM_END:V_END, :], (raised[j] * scale).astype(BF), 1, 0)
    out_ref[which, :, pl.ds(start, tile)] = result.astype(BF)
    wide_ref[which, :, pl.ds(start, tile)] = result
    lse_ref[which, :, pl.ds(start, tile)] = top + jnp.log(total)


def attend(qkv, tile):
    blocks, _, block = qkv.shape
    whole = lambda rows: pl.BlockSpec((blocks, rows, block), lambda i: (0, 0, 0))
    count = blocks * block
    return pl.pallas_call(
        functools.partial(attend_kernel, tile),
        grid=(count // tile,),
        in_specs=[whole(V_END)],
        out_specs=[whole(HD), whole(HD), whole(1)],
        out_shape=[
            jax.ShapeDtypeStruct((blocks, HD, block), BF),
            jax.ShapeDtypeStruct((blocks, HD, block), F32),
            jax.ShapeDtypeStruct((blocks, 1, block), F32),
        ],
        compiler_params=pltpu.CompilerParams(vmem_limit_bytes=40 << 20),
        cost_estimate=pl.CostEstimate(
            flops=count * count * HD * 8, bytes_accessed=count * 1024, transcendentals=count * count
        ),
        name="attend",
    )(qkv)


def attend_back_kernel(tile, qkv_ref, grad_ref, wide_ref, lse_ref, out_ref, sums):
    blocks, _, block = qkv_ref.shape
    per_block = block // tile
    step = pl.program_id(0)

    @pl.when(step == 0)
    def _():
        sums[...] = jnp.zeros_like(sums)

    which = step // per_block
    start = pl.multiple_of(step % per_block * tile, tile)
    query = qkv_ref[which, :QM_END, pl.ds(start, tile)]
    grad = grad_ref[which, :, pl.ds(start, tile)]
    delta = jnp.sum(
        grad.astype(F32) * wide_ref[which, :, pl.ds(start, tile)], axis=0, keepdims=True
    )
    lse = lse_ref[which, :, pl.ds(start, tile)]
    grad_query = jnp.zeros((HD, tile), F32)
    for j in range(blocks):
        prob = jnp.exp(dot(qkv_ref[j, QM_END:KM_END, :], query, 0, 0) - lse)
        grad_prob = dot(qkv_ref[j, KM_END:V_END, :], grad, 0, 0)
        grad_score = (prob * (grad_prob - delta)).astype(BF)
        grad_query += dot(qkv_ref[j, QM_END:K_END, :], grad_score, 1, 0)
        sums[j, :HD, :] += dot(query[:HD], grad_score, 1, 1)
        sums[j, HD:, :] += dot(grad, prob.astype(BF), 1, 1)
    out_ref[which, :HD, pl.ds(start, tile)] = (grad_query * 0.125).astype(BF)

    @pl.when(step == pl.num_programs(0) - 1)
    def _():
        out_ref[:, HD:, :] = sums[...].astype(BF)


def attend_back(qkv, grad, wide, lse, tile):
    blocks, _, block = qkv.shape
    whole = lambda rows: pl.BlockSpec((blocks, rows, block), lambda i: (0, 0, 0))
    count = blocks * block
    return pl.pallas_call(
        functools.partial(attend_back_kernel, tile),
        grid=(count // tile,),
        in_specs=[whole(V_END), whole(HD), whole(HD), whole(1)],
        out_specs=whole(3 * HD),
        out_shape=jax.ShapeDtypeStruct((blocks, 3 * HD, block), BF),
        scratch_shapes=[pltpu.VMEM((blocks, 2 * HD, block), F32)],
        compiler_params=pltpu.CompilerParams(vmem_limit_bytes=40 << 20),
        cost_estimate=pl.CostEstimate(
            flops=count * count * HD * 20, bytes_accessed=count * 1536, transcendentals=count * count
        ),
        name="attend_back",
    )(qkv, grad, wide, lse)


def body(tokens, d_out, segment_ids, position_ids, w_qkv, w_attn, w_in, w_out, gain_attn, gain_mlp):
    groups = lax.axis_size("heads")
    member = lax.axis_index("heads")
    rows, width = tokens.shape
    shard = w_qkv.shape[0]
    block = rows * groups
    reach = SEQ_MAX // block
    per_group = H // groups
    assert per_group == reach
    lanes = per_group * HD
    hidden = FF // groups
    padded = -(-hidden // 128) * 128
    tile = min(512, block)

    def swap(value, number):
        return exchange(value, "ctx", reach, True, number)

    def heads_gather(value, number):
        return exchange(value, "heads", groups, False, number)

    def own_rows(value):
        return lax.dynamic_slice_in_dim(value, member * rows, rows, 0)

    def heads_sum(value, number):
        parts = exchange(
            value.astype(BF).reshape(groups, rows, width), "heads", groups, True, number
        )
        return jnp.sum(parts.astype(F32), axis=0)

    extra = jnp.stack([position_ids // 256, position_ids % 256, segment_ids % 2], axis=1)
    extra = jnp.pad(extra.astype(BF), ((0, 0), (0, 125)))
    gathered_block = heads_gather(jnp.concatenate([tokens, d_out, extra], axis=1), 0).reshape(
        block, 2 * width + 128
    )
    qkv_part = lax.dynamic_slice_in_dim(
        w_qkv.reshape(shard, 3, width), member * lanes, lanes, 2
    ).reshape(shard, 3 * lanes)
    gains = jnp.pad(jnp.stack([gain_attn, gain_mlp], axis=1), ((0, 0), (0, 126)))
    attn_part = lax.dynamic_slice_in_dim(w_attn, member * lanes, lanes, 1)
    first_weights = lax.all_gather(
        jnp.concatenate([qkv_part, gains, attn_part], axis=1), "ctx", axis=0, tiled=True
    )

    def fit(value):
        return jnp.pad(value, ((0, 0), (0, padded - hidden)))

    left_part = fit(lax.dynamic_slice_in_dim(w_in, member * hidden, hidden, 1))
    right_part = fit(lax.dynamic_slice_in_dim(w_in, FF + member * hidden, hidden, 1))
    out_part = fit(lax.dynamic_slice_in_dim(w_out, member * hidden, hidden, 0).T)
    full_attn = (
        heads_gather(first_weights[:, 3 * lanes + 128 :], 12)
        .transpose(1, 0, 2)
        .reshape(width, width)
    )
    mlp_weights = lax.all_gather(
        jnp.concatenate([left_part, right_part, out_part], axis=1), "ctx", axis=0, tiled=True
    )
    in_weights = mlp_weights[:, : 2 * padded]
    out_weights = mlp_weights[:, 2 * padded :]

    residual_in = gathered_block[:, :width].astype(F32)
    upstream = gathered_block[:, width : 2 * width]
    digits = gathered_block[:, 2 * width :].astype(F32)
    positions = digits[:, 0] * 256.0 + digits[:, 1]
    parity = digits[:, 2][None, :]
    freqs = jnp.power(160000.0, -(2.0 * jnp.arange(HALF, dtype=F32)) / HD)
    angles = freqs[:, None] * positions[None, :]
    cosine = jnp.cos(angles)
    sine = jnp.sin(angles)

    qkv_weights = first_weights[:, : 3 * lanes]
    gain_one = first_weights[:, 3 * lanes].astype(F32)
    gain_two = first_weights[:, 3 * lanes + 1].astype(F32)
    plain_one, inverse_one = norm_parts(residual_in)
    attn_input = (plain_one * gain_one).astype(BF)
    projected = dot(qkv_weights, attn_input, 0, 1).reshape(3, per_group, 2, HALF, block)

    def turn(value):
        front, back = value[:, 0], value[:, 1]
        return jnp.concatenate([front * cosine - back * sine, back * cosine + front * sine], axis=1)

    def mark_rows(first, second):
        pad = jnp.zeros((MARKS - 2, block), F32)
        stacked = jnp.concatenate([first, second, pad], axis=0)
        return jnp.broadcast_to(stacked[None], (per_group, MARKS, block))

    outgoing = jnp.concatenate(
        [
            turn(projected[0]) * 0.125,
            mark_rows(parity, 1.0 - parity),
            turn(projected[1]),
            mark_rows((1.0 - parity) * MASKED, parity * MASKED),
            projected[2].reshape(per_group, HD, block),
        ],
        axis=1,
    ).astype(BF)
    qkv = swap(outgoing, 1)
    attended, attended_wide, lse = attend(qkv, tile)
    returned = swap(attended, 2).reshape(lanes, block)
    attended_all = heads_gather(returned, 3).reshape(width, block)
    middle = residual_in + dot(attended_all, full_attn, 0, 0)
    plain_two, inverse_two = norm_parts(middle)
    mlp_input = (plain_two * gain_two).astype(BF)
    gate_up = dot(mlp_input, in_weights, 1, 0)
    gate_left = gate_up[:, :padded]
    gate_right = gate_up[:, padded:]
    normal_cdf = 0.5 * (1.0 + lax.erf(gate_left * 0.7071067811865476))
    gelu = gate_left * normal_cdf
    density = jnp.exp(-0.5 * gate_left * gate_left) * 0.3989422804014327
    mixed = (gelu * gate_right).astype(BF)
    grad_mixed = dot(upstream, out_weights, 1, 0)
    grad_left = grad_mixed * gate_right * (normal_cdf + gate_left * density)
    grad_gate_up = jnp.concatenate([grad_left, grad_mixed * gelu], axis=1).astype(BF)
    grad_out_part = dot(upstream, mixed, 0, 0)
    grad_in_part = dot(mlp_input, grad_gate_up, 0, 0)
    late = lax.psum_scatter(
        jnp.concatenate([grad_in_part, grad_out_part], axis=1).astype(BF),
        "ctx",
        scatter_dimension=0,
        tiled=True,
    )
    grad_mlp_part = dot(grad_gate_up, in_weights, 1, 1)
    grad_gain_two = jnp.sum(grad_mlp_part * plain_two, axis=0)
    grad_norm_mid = norm_back(
        heads_sum(grad_mlp_part, 4), own_rows(plain_two), own_rows(inverse_two), gain_two
    )
    grad_middle = d_out.astype(F32) + grad_norm_mid
    grad_branch = heads_gather(grad_middle.astype(BF), 5).reshape(block, width)
    attn_rows = lax.dynamic_slice_in_dim(full_attn, member * lanes, lanes, 0)
    grad_attended = dot(attn_rows, grad_branch, 1, 1).astype(BF).reshape(per_group, HD, block)
    grad_heads = swap(grad_attended, 6)
    branch_columns = lax.dynamic_slice_in_dim(grad_branch, member * lanes, lanes, 1)
    grad_attn_part = dot(attended_all, branch_columns, 1, 0)
    grad_qkv = swap(attend_back(qkv, grad_heads, attended_wide, lse, tile), 7)
    grad_qkv = grad_qkv.astype(F32).reshape(per_group, 3, 2, HALF, block)

    def turn_back(value):
        front, back = value[:, 0], value[:, 1]
        return jnp.stack([front * cosine + back * sine, back * cosine - front * sine], axis=1)

    grad_projected = (
        jnp.stack([turn_back(grad_qkv[:, 0]), turn_back(grad_qkv[:, 1]), grad_qkv[:, 2]])
        .reshape(3 * lanes, block)
        .astype(BF)
    )
    grad_attn_in = dot(grad_projected, qkv_weights, 0, 1)
    grad_gain_one = jnp.sum(grad_attn_in * plain_one, axis=0)
    grad_qkv_part = dot(attn_input, grad_projected, 0, 1)
    grad_gains = jnp.pad(jnp.stack([grad_gain_one, grad_gain_two], axis=1), ((0, 0), (0, 126)))
    last_terms = jnp.concatenate([grad_qkv_part, grad_gains, grad_attn_part], axis=1).astype(BF)
    late, last_terms = lax.optimization_barrier((late, last_terms))
    last = lax.psum_scatter(
        last_terms,
        "ctx",
        scatter_dimension=0,
        tiled=True,
    )
    grad_input = grad_middle + norm_back(
        heads_sum(grad_attn_in, 8), own_rows(plain_one), own_rows(inverse_one), gain_one
    )
    mixed, _ = lax.optimization_barrier((mixed, grad_input))
    result = (own_rows(middle) + heads_sum(dot(mixed, out_weights, 1, 1), 9)).astype(BF)
    late_all = heads_gather(late, 10)
    last_all = heads_gather(last, 11)
    sum_qkv = (
        last_all[:, :, : 3 * lanes]
        .reshape(groups, shard, 3, lanes)
        .transpose(1, 2, 0, 3)
        .reshape(shard, 3 * width)
        .astype(F32)
    )
    gain_sums = jnp.sum(last_all[:, :, 3 * lanes : 3 * lanes + 2].astype(F32), axis=0)

    def columns(start, size, held=late_all):
        piece = held[:, :, start : start + size]
        return piece.transpose(1, 0, 2).reshape(shard, groups * size).astype(F32)

    sum_in = jnp.concatenate([columns(0, hidden), columns(padded, hidden)], axis=1)
    sum_out = (
        late_all[:, :, 2 * padded : 2 * padded + hidden]
        .transpose(0, 2, 1)
        .reshape(groups * hidden, shard)
        .astype(F32)
    )
    sum_attn = columns(3 * lanes + 128, lanes, last_all)
    return (
        result,
        grad_input,
        sum_qkv,
        sum_attn,
        sum_in,
        sum_out,
        gain_sums[:, 0],
        gain_sums[:, 1],
    )


def solution(mesh):
    return jax.shard_map(
        body,
        mesh=mesh,
        in_specs=(
            P(("ctx", "heads"), None),
            P(("ctx", "heads"), None),
            P(("ctx", "heads")),
            P(("ctx", "heads")),
            P("ctx", None),
            P("ctx", None),
            P("ctx", None),
            P(None, "ctx"),
            P("ctx"),
            P("ctx"),
        ),
        out_specs=(
            P(("ctx", "heads"), None),
            P(("ctx", "heads"), None),
            P("ctx", None),
            P("ctx", None),
            P("ctx", None),
            P(None, "ctx"),
            P("ctx"),
            P("ctx"),
        ),
        check_vma=False,
    )
```

```python
import functools

import jax
import jax.numpy as jnp
from jax import lax
from jax.experimental import pallas as pl
from jax.experimental.pallas import tpu as pltpu
from jax.sharding import PartitionSpec as P

H = 16
HD = 64
HALF = HD // 2
FF = 2624
SEQ_MAX = 2048
MASKED = -1e30
MARKS = 16
Q_END = HD
QM_END = Q_END + MARKS
K_END = QM_END + HD
KM_END = K_END + MARKS
V_END = KM_END + HD
BF = jnp.bfloat16
F32 = jnp.float32


def dot(left, right, left_dim, right_dim):
    return lax.dot_general(
        left, right, (((left_dim,), (right_dim,)), ((), ())), preferred_element_type=F32
    )


def exchange_kernel(count, axis, split, source, target, send, recv, local):
    place = lax.axis_index(axis)
    base = place // count * count
    me = place - base
    barrier = pltpu.get_barrier_semaphore()
    for step in range(1, count):
        peer = lax.rem(me + step, count)
        pl.semaphore_signal(
            barrier, inc=1, device_id={axis: base + peer}, device_id_type=pl.DeviceIdType.MESH
        )
    pl.semaphore_wait(barrier, count - 1)
    copies = []
    for step in range(1, count):
        peer = lax.rem(me + step, count)
        copy = pltpu.make_async_remote_copy(
            src_ref=source.at[peer] if split else source,
            dst_ref=target.at[me],
            send_sem=send.at[step - 1],
            recv_sem=recv.at[step - 1],
            device_id={axis: base + peer},
            device_id_type=pl.DeviceIdType.MESH,
        )
        copy.start()
        copies.append(copy)
    own = pltpu.make_async_copy(source.at[me] if split else source, target.at[me], local)
    own.start()
    own.wait()
    for copy in copies:
        copy.wait()


def paired_gather_kernel(count, axis, source, target, send, recv, local):
    me = lax.axis_index(axis)
    pair = me + 1 - 2 * lax.rem(me, 2)
    half = count // 2
    barrier = pltpu.get_barrier_semaphore()
    for peer in [pair] + [lax.rem(me + 2 * k, count) for k in range(1, half)]:
        pl.semaphore_signal(
            barrier, inc=1, device_id={axis: peer}, device_id_type=pl.DeviceIdType.MESH
        )
    pl.semaphore_wait(barrier, half)

    def push(piece, place, peer, at):
        copy = pltpu.make_async_remote_copy(
            src_ref=piece,
            dst_ref=target.at[place],
            send_sem=send.at[at],
            recv_sem=recv.at[at],
            device_id={axis: peer},
            device_id_type=pl.DeviceIdType.MESH,
        )
        copy.start()
        return copy

    far = [push(source, me, lax.rem(me + 2 * k, count), k) for k in range(1, half)]
    near = [push(source, me, pair, 0)]
    own = pltpu.make_async_copy(source, target.at[me], local)
    own.start()
    for k in range(1, half):
        far[k - 1].wait_recv()
        origin = lax.rem(me - 2 * k + count, count)
        near.append(push(target.at[origin], origin, pair, half - 1 + k))
    own.wait()
    for copy in far:
        copy.wait_send()
    for copy in near:
        copy.wait()


def exchange(value, axis, count, split, number):
    shape = value.shape if split else (count, *value.shape)
    moved = value.size * value.dtype.itemsize * (1 if split else count)
    return pl.pallas_call(
        functools.partial(exchange_kernel, count, axis, True)
        if split
        else functools.partial(paired_gather_kernel, count, axis),
        in_specs=[pl.BlockSpec(memory_space=pl.ANY)],
        out_specs=pl.BlockSpec(memory_space=pl.ANY),
        out_shape=jax.ShapeDtypeStruct(shape, value.dtype),
        scratch_shapes=[
            pltpu.SemaphoreType.DMA((count - 1,)),
            pltpu.SemaphoreType.DMA((count - 1,)),
            pltpu.SemaphoreType.DMA,
        ],
        compiler_params=pltpu.CompilerParams(collective_id=number, has_side_effects=True),
        cost_estimate=pl.CostEstimate(flops=0, bytes_accessed=moved, transcendentals=0),
        name=f"exchange_{number}",
    )(value)


def norm_parts(values):
    average = jnp.mean(values, axis=-1, keepdims=True)
    centred = values - average
    inverse_std = lax.rsqrt(jnp.mean(centred * centred, axis=-1, keepdims=True) + 1e-05)
    return centred * inverse_std, inverse_std


def norm_back(upstream, normed, inverse_std, gain):
    scaled = upstream * gain
    return inverse_std * (
        scaled
        - jnp.mean(scaled, axis=-1, keepdims=True)
        - normed * jnp.mean(scaled * normed, axis=-1, keepdims=True)
    )


def attend_kernel(tile, qkv_ref, out_ref, wide_ref, lse_ref):
    blocks, _, block = qkv_ref.shape
    per_block = block // tile
    step = pl.program_id(0)
    which = step // per_block
    start = pl.multiple_of(step % per_block * tile, tile)
    query = qkv_ref[which, :QM_END, pl.ds(start, tile)]
    scores = [dot(qkv_ref[j, QM_END:KM_END, :], query, 0, 0) for j in range(blocks)]
    top = functools.reduce(jnp.maximum, [jnp.max(s, axis=0, keepdims=True) for s in scores])
    raised = [jnp.exp(s - top) for s in scores]
    total = functools.reduce(jnp.add, [jnp.sum(e, axis=0, keepdims=True) for e in raised])
    scale = 1.0 / total
    result = jnp.zeros((HD, tile), F32)
    for j in range(blocks):
        result += dot(qkv_ref[j, KM_END:V_END, :], (raised[j] * scale).astype(BF), 1, 0)
    out_ref[which, :, pl.ds(start, tile)] = result.astype(BF)
    wide_ref[which, :, pl.ds(start, tile)] = result
    lse_ref[which, :, pl.ds(start, tile)] = top + jnp.log(total)


def attend(qkv, tile):
    blocks, _, block = qkv.shape
    whole = lambda rows: pl.BlockSpec((blocks, rows, block), lambda i: (0, 0, 0))
    count = blocks * block
    return pl.pallas_call(
        functools.partial(attend_kernel, tile),
        grid=(count // tile,),
        in_specs=[whole(V_END)],
        out_specs=[whole(HD), whole(HD), whole(1)],
        out_shape=[
            jax.ShapeDtypeStruct((blocks, HD, block), BF),
            jax.ShapeDtypeStruct((blocks, HD, block), F32),
            jax.ShapeDtypeStruct((blocks, 1, block), F32),
        ],
        compiler_params=pltpu.CompilerParams(vmem_limit_bytes=40 << 20),
        cost_estimate=pl.CostEstimate(
            flops=count * count * HD * 8, bytes_accessed=count * 1024, transcendentals=count * count
        ),
        name="attend",
    )(qkv)


def attend_back_kernel(tile, qkv_ref, grad_ref, wide_ref, lse_ref, out_ref, sums):
    blocks, _, block = qkv_ref.shape
    per_block = block // tile
    step = pl.program_id(0)

    @pl.when(step == 0)
    def _():
        sums[...] = jnp.zeros_like(sums)

    which = step // per_block
    start = pl.multiple_of(step % per_block * tile, tile)
    query = qkv_ref[which, :QM_END, pl.ds(start, tile)]
    grad = grad_ref[which, :, pl.ds(start, tile)]
    delta = jnp.sum(
        grad.astype(F32) * wide_ref[which, :, pl.ds(start, tile)], axis=0, keepdims=True
    )
    lse = lse_ref[which, :, pl.ds(start, tile)]
    grad_query = jnp.zeros((HD, tile), F32)
    for j in range(blocks):
        prob = jnp.exp(dot(qkv_ref[j, QM_END:KM_END, :], query, 0, 0) - lse)
        grad_prob = dot(qkv_ref[j, KM_END:V_END, :], grad, 0, 0)
        grad_score = (prob * (grad_prob - delta)).astype(BF)
        grad_query += dot(qkv_ref[j, QM_END:K_END, :], grad_score, 1, 0)
        sums[j, :HD, :] += dot(query[:HD], grad_score, 1, 1)
        sums[j, HD:, :] += dot(grad, prob.astype(BF), 1, 1)
    out_ref[which, :HD, pl.ds(start, tile)] = (grad_query * 0.125).astype(BF)

    @pl.when(step == pl.num_programs(0) - 1)
    def _():
        out_ref[:, HD:, :] = sums[...].astype(BF)


def attend_back(qkv, grad, wide, lse, tile):
    blocks, _, block = qkv.shape
    whole = lambda rows: pl.BlockSpec((blocks, rows, block), lambda i: (0, 0, 0))
    count = blocks * block
    return pl.pallas_call(
        functools.partial(attend_back_kernel, tile),
        grid=(count // tile,),
        in_specs=[whole(V_END), whole(HD), whole(HD), whole(1)],
        out_specs=whole(3 * HD),
        out_shape=jax.ShapeDtypeStruct((blocks, 3 * HD, block), BF),
        scratch_shapes=[pltpu.VMEM((blocks, 2 * HD, block), F32)],
        compiler_params=pltpu.CompilerParams(vmem_limit_bytes=40 << 20),
        cost_estimate=pl.CostEstimate(
            flops=count * count * HD * 20, bytes_accessed=count * 1536, transcendentals=count * count
        ),
        name="attend_back",
    )(qkv, grad, wide, lse)


def body(tokens, d_out, segment_ids, position_ids, w_qkv, w_attn, w_in, w_out, gain_attn, gain_mlp):
    groups = lax.axis_size("heads")
    member = lax.axis_index("heads")
    rows, width = tokens.shape
    shard = w_qkv.shape[0]
    block = rows * groups
    reach = SEQ_MAX // block
    per_group = H // groups
    assert per_group == reach
    lanes = per_group * HD
    hidden = FF // groups
    padded = -(-hidden // 128) * 128
    tile = min(512, block)

    def swap(value, number):
        return exchange(value, "ctx", reach, True, number)

    def heads_gather(value, number):
        return exchange(value, "heads", groups, False, number)

    def own_rows(value):
        return lax.dynamic_slice_in_dim(value, member * rows, rows, 0)

    def heads_sum(value, number):
        parts = exchange(
            value.astype(BF).reshape(groups, rows, width), "heads", groups, True, number
        )
        return jnp.sum(parts.astype(F32), axis=0)

    extra = jnp.stack([position_ids // 256, position_ids % 256, segment_ids % 2], axis=1)
    extra = jnp.pad(extra.astype(BF), ((0, 0), (0, 125)))
    gathered_block = heads_gather(jnp.concatenate([tokens, d_out, extra], axis=1), 0).reshape(
        block, 2 * width + 128
    )
    qkv_part = lax.dynamic_slice_in_dim(
        w_qkv.reshape(shard, 3, width), member * lanes, lanes, 2
    ).reshape(shard, 3 * lanes)
    gains = jnp.pad(jnp.stack([gain_attn, gain_mlp], axis=1), ((0, 0), (0, 126)))
    attn_part = lax.dynamic_slice_in_dim(w_attn, member * lanes, lanes, 1)
    first_weights = lax.all_gather(
        jnp.concatenate([qkv_part, gains, attn_part], axis=1), "ctx", axis=0, tiled=True
    )

    def fit(value):
        return jnp.pad(value, ((0, 0), (0, padded - hidden)))

    left_part = fit(lax.dynamic_slice_in_dim(w_in, member * hidden, hidden, 1))
    right_part = fit(lax.dynamic_slice_in_dim(w_in, FF + member * hidden, hidden, 1))
    out_part = fit(lax.dynamic_slice_in_dim(w_out, member * hidden, hidden, 0).T)
    full_attn = (
        heads_gather(first_weights[:, 3 * lanes + 128 :], 12)
        .transpose(1, 0, 2)
        .reshape(width, width)
    )
    mlp_weights = lax.all_gather(
        jnp.concatenate([left_part, right_part, out_part], axis=1), "ctx", axis=0, tiled=True
    )
    in_weights = mlp_weights[:, : 2 * padded]
    out_weights = mlp_weights[:, 2 * padded :]

    residual_in = gathered_block[:, :width].astype(F32)
    upstream = gathered_block[:, width : 2 * width]
    digits = gathered_block[:, 2 * width :].astype(F32)
    positions = digits[:, 0] * 256.0 + digits[:, 1]
    parity = digits[:, 2][None, :]
    freqs = jnp.power(160000.0, -(2.0 * jnp.arange(HALF, dtype=F32)) / HD)
    angles = freqs[:, None] * positions[None, :]
    cosine = jnp.cos(angles)
    sine = jnp.sin(angles)

    qkv_weights = first_weights[:, : 3 * lanes]
    gain_one = first_weights[:, 3 * lanes].astype(F32)
    gain_two = first_weights[:, 3 * lanes + 1].astype(F32)
    plain_one, inverse_one = norm_parts(residual_in)
    attn_input = (plain_one * gain_one).astype(BF)
    projected = dot(qkv_weights, attn_input, 0, 1).reshape(3, per_group, 2, HALF, block)

    def turn(value):
        front, back = value[:, 0], value[:, 1]
        return jnp.concatenate([front * cosine - back * sine, back * cosine + front * sine], axis=1)

    def mark_rows(first, second):
        pad = jnp.zeros((MARKS - 2, block), F32)
        stacked = jnp.concatenate([first, second, pad], axis=0)
        return jnp.broadcast_to(stacked[None], (per_group, MARKS, block))

    outgoing = jnp.concatenate(
        [
            turn(projected[0]) * 0.125,
            mark_rows(parity, 1.0 - parity),
            turn(projected[1]),
            mark_rows((1.0 - parity) * MASKED, parity * MASKED),
            projected[2].reshape(per_group, HD, block),
        ],
        axis=1,
    ).astype(BF)
    qkv = swap(outgoing, 1)
    attended, attended_wide, lse = attend(qkv, tile)
    returned = swap(attended, 2).reshape(lanes, block)
    attended_all = heads_gather(returned, 3).reshape(width, block)
    middle = residual_in + dot(attended_all, full_attn, 0, 0)
    plain_two, inverse_two = norm_parts(middle)
    mlp_input = (plain_two * gain_two).astype(BF)
    gate_up = dot(mlp_input, in_weights, 1, 0)
    gate_left = gate_up[:, :padded]
    gate_right = gate_up[:, padded:]
    normal_cdf = 0.5 * (1.0 + lax.erf(gate_left * 0.7071067811865476))
    gelu = gate_left * normal_cdf
    density = jnp.exp(-0.5 * gate_left * gate_left) * 0.3989422804014327
    mixed = (gelu * gate_right).astype(BF)
    grad_mixed = dot(upstream, out_weights, 1, 0)
    grad_left = grad_mixed * gate_right * (normal_cdf + gate_left * density)
    grad_gate_up = jnp.concatenate([grad_left, grad_mixed * gelu], axis=1).astype(BF)
    grad_out_part = dot(upstream, mixed, 0, 0)
    grad_in_part = dot(mlp_input, grad_gate_up, 0, 0)
    late = lax.psum_scatter(
        jnp.concatenate([grad_in_part, grad_out_part], axis=1).astype(BF),
        "ctx",
        scatter_dimension=0,
        tiled=True,
    )
    grad_mlp_part = dot(grad_gate_up, in_weights, 1, 1)
    grad_gain_two = jnp.sum(grad_mlp_part * plain_two, axis=0)
    grad_norm_mid = norm_back(
        heads_sum(grad_mlp_part, 4), own_rows(plain_two), own_rows(inverse_two), gain_two
    )
    grad_middle = d_out.astype(F32) + grad_norm_mid
    grad_branch = heads_gather(grad_middle.astype(BF), 5).reshape(block, width)
    attn_rows = lax.dynamic_slice_in_dim(full_attn, member * lanes, lanes, 0)
    grad_attended = dot(attn_rows, grad_branch, 1, 1).astype(BF).reshape(per_group, HD, block)
    grad_heads = swap(grad_attended, 6)
    branch_columns = lax.dynamic_slice_in_dim(grad_branch, member * lanes, lanes, 1)
    grad_attn_part = dot(attended_all, branch_columns, 1, 0)
    grad_qkv = swap(attend_back(qkv, grad_heads, attended_wide, lse, tile), 7)
    grad_qkv = grad_qkv.astype(F32).reshape(per_group, 3, 2, HALF, block)

    def turn_back(value):
        front, back = value[:, 0], value[:, 1]
        return jnp.stack([front * cosine + back * sine, back * cosine - front * sine], axis=1)

    grad_projected = (
        jnp.stack([turn_back(grad_qkv[:, 0]), turn_back(grad_qkv[:, 1]), grad_qkv[:, 2]])
        .reshape(3 * lanes, block)
        .astype(BF)
    )
    grad_attn_in = dot(grad_projected, qkv_weights, 0, 1)
    grad_gain_one = jnp.sum(grad_attn_in * plain_one, axis=0)
    grad_qkv_part = dot(attn_input, grad_projected, 0, 1)
    grad_gains = jnp.pad(jnp.stack([grad_gain_one, grad_gain_two], axis=1), ((0, 0), (0, 126)))
    last_terms = jnp.concatenate([grad_qkv_part, grad_gains, grad_attn_part], axis=1).astype(BF)
    late, last_terms = lax.optimization_barrier((late, last_terms))
    last = lax.psum_scatter(
        last_terms,
        "ctx",
        scatter_dimension=0,
        tiled=True,
    )
    grad_input = grad_middle + norm_back(
        heads_sum(grad_attn_in, 8), own_rows(plain_one), own_rows(inverse_one), gain_one
    )
    mixed, _ = lax.optimization_barrier((mixed, grad_input))
    result = (own_rows(middle) + heads_sum(dot(mixed, out_weights, 1, 1), 9)).astype(BF)
    late_all = heads_gather(late, 10)
    last_all = heads_gather(last, 11)
    sum_qkv = (
        last_all[:, :, : 3 * lanes]
        .reshape(groups, shard, 3, lanes)
        .transpose(1, 2, 0, 3)
        .reshape(shard, 3 * width)
        .astype(F32)
    )
    gain_sums = jnp.sum(last_all[:, :, 3 * lanes : 3 * lanes + 2].astype(F32), axis=0)

    def columns(start, size, held=late_all):
        piece = held[:, :, start : start + size]
        return piece.transpose(1, 0, 2).reshape(shard, groups * size).astype(F32)

    sum_in = jnp.concatenate([columns(0, hidden), columns(padded, hidden)], axis=1)
    sum_out = (
        late_all[:, :, 2 * padded : 2 * padded + hidden]
        .transpose(0, 2, 1)
        .reshape(groups * hidden, shard)
        .astype(F32)
    )
    sum_attn = columns(3 * lanes + 128, lanes, last_all)
    return (
        result,
        grad_input,
        sum_qkv,
        sum_attn,
        sum_in,
        sum_out,
        gain_sums[:, 0],
        gain_sums[:, 1],
    )


def solution(mesh):
    return jax.shard_map(
        body,
        mesh=mesh,
        in_specs=(
            P(("ctx", "heads"), None),
            P(("ctx", "heads"), None),
            P(("ctx", "heads")),
            P(("ctx", "heads")),
            P("ctx", None),
            P("ctx", None),
            P("ctx", None),
            P(None, "ctx"),
            P("ctx"),
            P("ctx"),
        ),
        out_specs=(
            P(("ctx", "heads"), None),
            P(("ctx", "heads"), None),
            P("ctx", None),
            P("ctx", None),
            P("ctx", None),
            P(None, "ctx"),
            P("ctx"),
            P("ctx"),
        ),
        check_vma=False,
    )
```
